512 devices in a mesh: item: 16 (over y, core), user: 32 (over z, x).
Axes of the slice: x: 4, y: 8, z: 8, core: 2. Of those that a mesh axis runs over, the one named last changes fastest.
Arguments:
- item_factors: float32 [32768, 128], P('item')
- tile_lists: int32 [512, 16], P(('item', 'user')), may hold values from 0 to 255, as said below
- tile_weights: bfloat16 [512, 16, 128, 128], P(('item', 'user')), may hold values from 0 to 40
- user_factors: float32 [65536, 128], P(('item', 'user')), may hold values from -6 to 6
Outputs:
- new_factors: float32 [65536, 128], P(('item', 'user'))
The draws below stay inside these ranges and needn't reach their ends.
Inputs may be any that keep to these rules, and one draw needn't show every extreme that they name: `tile_lists`: item shard s holds tiles s * 16 to (s + 1) * 16 - 1. Among the 16 slots of one device's blocks, at most 2 name tiles of one item shard, and for some shard exactly 2 do; a tile may be named more than once.
All inputs are finite; a program needn't handle non-finite values.
Results may differ from the reference program's by a relative error of at most 0.0024.
Values sent between devices are 32-bit elements; how exact they have to be, the bound alone decides.
No kernel may reach another device: no remote copies, remote signals or barrier semaphores. Data moves between devices by JAX's collectives and lax.ppermute only.
A program may use at most 64 MiB of HBM per device.

```python
import math
import jax
import jax.numpy as jnp
from jax import lax

R = 128
TILE = 128
BLK_DEV = 1
K = 16
ITILES_DEV = 16
ITERS = 4
BLOCKS = 512
USERS = 65536
ITEM_TILES = 256
ITEMS = 32768


def draw_item_factors(key, part):
    first, second, third = jax.random.split(key, 3)
    base = jax.random.normal(first, (ITEMS, R), jnp.float32)
    columns = jnp.exp(jax.random.uniform(second, (1, R), jnp.float32, math.log(0.3), math.log(3.0)))
    rising = jnp.sqrt(1.0 + 2.0 * jnp.arange(ITEMS, dtype=jnp.float32)[:, None] / ITEMS)
    row_scale = jnp.exp(jax.random.uniform(third, (ITEMS, 1), jnp.float32, math.log(0.3), math.log(3.0))) * rising
    return (base * row_scale * columns * (1.0 / math.sqrt(ITEMS))).astype(jnp.float32)


def draw_tile_lists(key, part):
    devices_total = BLOCKS // BLK_DEV
    slots_total = BLK_DEV * K
    shards_total = ITEM_TILES // ITILES_DEV
    capacity = 2 * slots_total // shards_total

    def device_list(dev_key):
        hot_key, pool_key, order_key, pick_key = jax.random.split(dev_key, 4)
        hot_shard = jax.random.randint(hot_key, (), 0, shards_total)
        pool = jax.random.permutation(pool_key, (shards_total - 1) * capacity)[:slots_total - capacity]
        others = pool // capacity
        others = jnp.where(others >= hot_shard, others + 1, others)
        owners = jnp.concatenate([jnp.full((capacity,), hot_shard, jnp.int32), others.astype(jnp.int32)])
        owners = owners[jax.random.permutation(order_key, slots_total)]
        offsets = jax.random.randint(pick_key, (slots_total,), 0, ITILES_DEV)
        return (owners * ITILES_DEV + offsets).astype(jnp.int32)
    keys = jax.random.split(jax.random.fold_in(key, 7), devices_total)
    return jax.vmap(device_list)(keys).reshape(BLOCKS, K)


def shard_levels(key, shape, pieces, least, high):
    gain = 1.0
    for axis_at, parts in pieces:
        steps = jax.random.uniform(jax.random.fold_in(jax.random.fold_in(key, 6), axis_at), (parts,), jnp.float32, least / len(pieces), high / len(pieces))
        gain = gain * jnp.repeat(jnp.exp(steps), shape[axis_at] // parts).reshape((-1,) + (1,) * (len(shape) - 1 - axis_at))
    return gain


def scatter_about(key, extent, deviation, bound, pieces=(), kind=jnp.bfloat16):
    loudness = shard_levels(key, extent, pieces, -0.22, 0.18) if pieces else 1.0
    drawn = jax.random.normal(key, extent, jnp.float32) * deviation * loudness
    return jnp.minimum(jnp.maximum(drawn, -bound), bound).astype(kind)


def setup_inputs(seed: int = 0) -> dict:
    streams_of = jax.random.split(jax.random.key(seed), 5)
    return {
        "item_factors": draw_item_factors(jax.random.fold_in(streams_of[4], 71), 0),
        "tile_lists": draw_tile_lists(jax.random.fold_in(streams_of[4], 71), 0),
        "tile_weights": jnp.clip(40.0 * jax.random.uniform(streams_of[2], (BLOCKS, K, TILE, TILE), jnp.float32) ** shard_levels(streams_of[2], (BLOCKS, K, TILE, TILE), ((0, 512),), -0.2, 0.2), 0.0, 40.0).astype(jnp.bfloat16),
        "user_factors": scatter_about(streams_of[3], (USERS, R), 1.0, 6.0, ((0, 512),), jnp.float32),
    }


RIDGE_WEIGHT = 0.1
EPSILON = 1e-6
HIGHEST = lax.Precision.HIGHEST


def apply_system(vectors, tiles, weights, gram):
    scores = jnp.einsum('bur,bkir->bkui', vectors, tiles, precision=HIGHEST)
    spread = jnp.einsum('bkui,bkir->bur', scores * weights, tiles, precision=HIGHEST)
    return spread + jnp.einsum('bur,rs->bus', vectors, gram, precision=HIGHEST) + RIDGE_WEIGHT * vectors


def conjugate(start, tiles, weights, gram, steps):
    weights = weights.astype(jnp.float32)
    target = jnp.einsum('bkui,bkir->bur', 1.0 + weights, tiles, precision=HIGHEST)
    answer = start
    resid = target - apply_system(start, tiles, weights, gram)
    direction = resid
    norm_now = jnp.sum(resid * resid, axis=-1, keepdims=True)
    for step_index in range(steps):
        image = apply_system(direction, tiles, weights, gram)
        alpha = norm_now / (jnp.sum(direction * image, axis=-1, keepdims=True) + EPSILON)
        answer = answer + alpha * direction
        resid = resid - alpha * image
        norm_next = jnp.sum(resid * resid, axis=-1, keepdims=True)
        direction = resid + (norm_next / (norm_now + EPSILON)) * direction
        norm_now = norm_next
    return answer


def reference(item_factors, tile_lists, tile_weights, user_factors):
    gram = jnp.dot(item_factors.T, item_factors, precision=HIGHEST, preferred_element_type=jnp.float32)
    all_tiles = item_factors.reshape(ITEM_TILES, TILE, R)

    def block_solve(packed):
        tile_ids, weights, start = packed
        tiles = all_tiles[tile_ids][None]
        return conjugate(start[None], tiles, weights[None], gram, ITERS)[0]

    solved = lax.map(block_solve, (tile_lists, tile_weights, user_factors.reshape(BLOCKS, TILE, R)))
    return solved.reshape(USERS, R)
```

```python
import jax
import jax.numpy as jnp
from jax import lax
from jax.experimental import pallas as pl
from jax.experimental.pallas import tpu as pltpu
from jax.sharding import PartitionSpec as P

ITERS = 4
RIDGE_WEIGHT = 0.1
EPSILON = 1e-06
TILE = 128
NEAR = 8
SLICE = TILE // NEAR


def halves(x):
    high = x.astype(jnp.bfloat16)
    low = (x - high.astype(jnp.float32)).astype(jnp.bfloat16)
    return high, low


def quadrants(x):
    rows, cols = x.shape[0] // 2, x.shape[1] // 2
    return (x[:rows, :cols] + x[:rows, cols:]) + (x[rows:, :cols] + x[rows:, cols:])


def prep_kernel(place_ref, shard_ref, out_ref, gram_ref):
    start = pl.multiple_of(place_ref[0] * SLICE, SLICE)
    tiles = shard_ref.shape[0] // TILE
    high, low = halves(shard_ref[...])
    both = jnp.concatenate([high, low], axis=1)
    gram_ref[...] = quadrants(
        lax.dot_general(both, both, (((0,), (0,)), ((), ())), preferred_element_type=jnp.float32)
    )
    pieces = [shard_ref[pl.ds(t * TILE + start, SLICE), :] for t in range(tiles)]
    pieces.append(gram_ref[pl.ds(start, SLICE), :])
    for t, piece in enumerate(pieces):
        for d in range(out_ref.shape[0]):
            out_ref[d, t * SLICE:(t + 1) * SLICE, :] = piece


def pick_kernel(core_ref, lists_ref, mine_ref, other_ref, out_ref):
    near, slots = lists_ref.shape
    core = core_ref[0]
    held = mine_ref.shape[1] // SLICE - 1
    last = held * SLICE
    gram = mine_ref[0, last:, :] + other_ref[0, last:, :]
    for y in range(1, mine_ref.shape[0]):
        gram = gram + (mine_ref[y, last:, :] + other_ref[y, last:, :])

    def one(d, _):
        for k in range(slots):
            tile = lists_ref[d, k]
            shard = tile // held
            row = shard // 2
            at = pl.multiple_of((tile - shard * held) * SLICE, SLICE)
            same = (shard - row * 2) == core
            a = mine_ref[row, pl.ds(at, SLICE), :]
            b = other_ref[row, pl.ds(at, SLICE), :]
            out_ref[d, k * SLICE:(k + 1) * SLICE, :] = jnp.where(same, a, b)
        out_ref[d, slots * SLICE:, :] = gram
        return 0

    lax.fori_loop(0, near, one, 0)


def solve_kernel(tiles_ref, weights_ref, start_ref, out_ref, y_ref, resid_ref, dir_ref):
    near = tiles_ref.shape[0]
    slots = weights_ref.shape[0]
    items = slots * TILE
    chunk = 2 * TILE

    for k in range(slots + 1):
        for p in range(near):
            high, low = halves(tiles_ref[p, k * SLICE:(k + 1) * SLICE, :])
            at = k * TILE + p * SLICE
            y_ref[at:at + SLICE, :TILE] = high
            y_ref[at:at + SLICE, TILE:] = low

    def wide(n):
        return jnp.concatenate([weights_ref[2 * n], weights_ref[2 * n + 1]], axis=1)

    def apply(v):
        high, low = halves(v)
        left = jnp.concatenate(
            [jnp.concatenate([high, high], axis=1), jnp.concatenate([low, low], axis=1)], axis=0
        )
        total = None
        for n in range(items // chunk):
            rows = y_ref[n * chunk:(n + 1) * chunk, :]
            s = lax.dot_general(left, rows, (((1,), (1,)), ((), ())), preferred_element_type=jnp.float32)
            scores = (s[:TILE] + s[TILE:]) * wide(n).astype(jnp.float32)
            part = jnp.dot(
                jnp.concatenate(halves(scores), axis=0), rows, preferred_element_type=jnp.float32
            )
            total = part if total is None else total + part
        g = lax.dot_general(
            left, y_ref[items:, :], (((1,), (1,)), ((), ())), preferred_element_type=jnp.float32
        )
        return quadrants(total) + (g[:TILE] + g[TILE:]) + RIDGE_WEIGHT * v

    ones = jnp.ones((16, chunk), jnp.bfloat16)
    total = None
    for n in range(items // chunk):
        part = jnp.dot(
            jnp.concatenate([wide(n), ones], axis=0),
            y_ref[n * chunk:(n + 1) * chunk, :],
            preferred_element_type=jnp.float32,
        )
        total = part if total is None else total + part
    total = total[:, :TILE] + total[:, TILE:]
    target = total[:TILE] + total[TILE:TILE + 1]

    start = start_ref[...]
    resid = target - apply(start)
    out_ref[...] = start
    resid_ref[...] = resid
    dir_ref[...] = resid

    def step(_, norm_now):
        direction = dir_ref[...]
        image = apply(direction)
        alpha = norm_now / (jnp.sum(direction * image, axis=-1, keepdims=True) + EPSILON)
        out_ref[...] = out_ref[...] + alpha * direction
        resid = resid_ref[...] - alpha * image
        norm_next = jnp.sum(resid * resid, axis=-1, keepdims=True)
        resid_ref[...] = resid
        dir_ref[...] = resid + norm_next / (norm_now + EPSILON) * direction
        return norm_next

    lax.fori_loop(0, ITERS, step, jnp.sum(resid * resid, axis=-1, keepdims=True))


VMEM = pl.BlockSpec(memory_space=pltpu.VMEM)
SMEM = pl.BlockSpec(memory_space=pltpu.SMEM)


def local(item_factors, tile_lists, tile_weights, user_factors):
    rank = item_factors.shape[1]
    slots = tile_lists.shape[1]
    shards = lax.axis_size("item")
    users = lax.axis_size("user")
    rows_y = shards // 2
    column = [[2 * y + c for y in range(rows_y)] for c in range(2)]
    around = [[g * NEAR + j for j in range(NEAR)] for g in range(users // NEAR)]
    swap = [(i, i ^ 1) for i in range(shards)]
    place = (lax.axis_index("user") % NEAR).astype(jnp.int32).reshape(1)
    core = (lax.axis_index("item") % 2).astype(jnp.int32).reshape(1)
    held = item_factors.shape[0] // TILE

    send_a, _ = pl.pallas_call(
        prep_kernel,
        out_shape=(
            jax.ShapeDtypeStruct((rows_y, (held + 1) * SLICE, rank), jnp.float32),
            jax.ShapeDtypeStruct((rank, rank), jnp.float32),
        ),
        in_specs=[SMEM, VMEM],
        out_specs=(VMEM, VMEM),
        name="prep",
    )(place, item_factors)
    with jax.named_scope("column"):
        mine = lax.all_to_all(send_a, "item", 0, 0, tiled=True, axis_index_groups=column)
    with jax.named_scope("lists"):
        near_lists = lax.all_to_all(
            jnp.broadcast_to(tile_lists, (NEAR, slots)), "user", 0, 0, tiled=True, axis_index_groups=around
        )
    with jax.named_scope("swap"):
        other = lax.ppermute(mine, "item", swap)
    send_b = pl.pallas_call(
        pick_kernel,
        out_shape=jax.ShapeDtypeStruct((NEAR, (slots + 1) * SLICE, rank), jnp.float32),
        in_specs=[SMEM, SMEM, VMEM, VMEM],
        out_specs=VMEM,
        name="pick",
    )(core, near_lists, mine, other)
    with jax.named_scope("around"):
        tiles = lax.all_to_all(send_b, "user", 0, 0, tiled=True, axis_index_groups=around)
    return pl.pallas_call(
        solve_kernel,
        out_shape=jax.ShapeDtypeStruct((TILE, rank), jnp.float32),
        in_specs=[VMEM, VMEM, VMEM],
        out_specs=VMEM,
        scratch_shapes=[
            pltpu.VMEM(((slots + 1) * TILE, 2 * rank), jnp.bfloat16),
            pltpu.VMEM((TILE, rank), jnp.float32),
            pltpu.VMEM((TILE, rank), jnp.float32),
        ],
        name="solve",
    )(tiles, tile_weights[0], user_factors)


def solution(mesh):
    in_specs = (
        P("item", None),
        P(("item", "user"), None),
        P(("item", "user"), None, None, None),
        P(("item", "user"), None),
    )
    out_specs = P(("item", "user"), None)
    return jax.shard_map(local, mesh=mesh, in_specs=in_specs, out_specs=out_specs, check_vma=False)
```

```python
import jax
import jax.numpy as jnp
from jax import lax
from jax.experimental import pallas as pl
from jax.experimental.pallas import tpu as pltpu
from jax.sharding import PartitionSpec as P


ITERS = 4
RIDGE_WEIGHT = 0.1
EPSILON = 1e-06
TILE = 128
NEAR = 8
SLICE = TILE // NEAR


def halves(x):
    high = x.astype(jnp.bfloat16)
    low = (x - high.astype(jnp.float32)).astype(jnp.bfloat16)
    return high, low


def quadrants(x):
    rows, cols = x.shape[0] // 2, x.shape[1] // 2
    return (x[:rows, :cols] + x[:rows, cols:]) + (x[rows:, :cols] + x[rows:, cols:])


def prep_kernel(place_ref, shard_ref, out_ref, gram_ref):
    start = pl.multiple_of(place_ref[0] * SLICE, SLICE)
    tiles = shard_ref.shape[0] // TILE
    high, low = halves(shard_ref[...])
    both = jnp.concatenate([high, low], axis=1)
    gram_ref[...] = quadrants(
        lax.dot_general(both, both, (((0,), (0,)), ((), ())), preferred_element_type=jnp.float32)
    )
    pieces = [shard_ref[pl.ds(t * TILE + start, SLICE), :] for t in range(tiles)]
    pieces.append(gram_ref[pl.ds(start, SLICE), :])
    for t, piece in enumerate(pieces):
        for d in range(out_ref.shape[0]):
            out_ref[d, t * SLICE:(t + 1) * SLICE, :] = piece


def pick_kernel(core_ref, place_ref, lists_ref, mine_ref, other_ref, out_ref):
    near, slots = lists_ref.shape
    core, place = core_ref[0], place_ref[0]
    held = mine_ref.shape[1] // SLICE - 1
    last = held * SLICE
    gram = mine_ref[0, last:, :] + other_ref[0, last:, :]
    for y in range(1, mine_ref.shape[0]):
        gram = gram + (mine_ref[y, last:, :] + other_ref[y, last:, :])

    def one(d, _):
        to = place ^ d
        for k in range(slots):
            tile = lists_ref[d, k]
            shard = tile >> (held.bit_length() - 1)
            row = shard >> 1
            at = pl.multiple_of((tile & (held - 1)) * SLICE, SLICE)
            a = mine_ref[row, pl.ds(at, SLICE), :]
            b = other_ref[row, pl.ds(at, SLICE), :]
            out_ref[to, k * SLICE:(k + 1) * SLICE, :] = jnp.where((shard & 1) == core, a, b)
        out_ref[to, slots * SLICE:, :] = gram
        return 0

    lax.fori_loop(0, near, one, 0)


def solve_kernel(tiles_ref, weights_ref, start_ref, out_ref, y_ref, resid_ref, dir_ref):
    near = tiles_ref.shape[0]
    slots = weights_ref.shape[0]
    items = slots * TILE
    chunk = 2 * TILE

    for k in range(slots + 1):
        for p in range(near):
            high, low = halves(tiles_ref[p, k * SLICE:(k + 1) * SLICE, :])
            at = k * TILE + p * SLICE
            y_ref[at:at + SLICE, :TILE] = high
            y_ref[at:at + SLICE, TILE:] = low

    def wide(n):
        return jnp.concatenate([weights_ref[2 * n], weights_ref[2 * n + 1]], axis=1)

    def apply(v):
        high, low = halves(v)
        left = jnp.concatenate(
            [jnp.concatenate([high, high], axis=1), jnp.concatenate([low, low], axis=1)], axis=0
        )
        total = None
        for n in range(items // chunk):
            rows = y_ref[n * chunk:(n + 1) * chunk, :]
            s = lax.dot_general(left, rows, (((1,), (1,)), ((), ())), preferred_element_type=jnp.float32)
            scores = (s[:TILE] + s[TILE:]) * wide(n).astype(jnp.float32)
            part = jnp.dot(
                jnp.concatenate(halves(scores), axis=0), rows, preferred_element_type=jnp.float32
            )
            total = part if total is None else total + part
        g = lax.dot_general(
            left, y_ref[items:, :], (((1,), (1,)), ((), ())), preferred_element_type=jnp.float32
        )
        return quadrants(total) + (g[:TILE] + g[TILE:]) + RIDGE_WEIGHT * v

    ones = jnp.ones((16, chunk), jnp.bfloat16)
    total = None
    for n in range(items // chunk):
        part = jnp.dot(
            jnp.concatenate([wide(n), ones], axis=0),
            y_ref[n * chunk:(n + 1) * chunk, :],
            preferred_element_type=jnp.float32,
        )
        total = part if total is None else total + part
    total = total[:, :TILE] + total[:, TILE:]
    target = total[:TILE] + total[TILE:TILE + 1]

    start = start_ref[...]
    resid = target - apply(start)
    out_ref[...] = start
    resid_ref[...] = resid
    dir_ref[...] = resid

    def step(_, norm_now):
        direction = dir_ref[...]
        image = apply(direction)
        alpha = norm_now / (jnp.sum(direction * image, axis=-1, keepdims=True) + EPSILON)
        out_ref[...] = out_ref[...] + alpha * direction
        resid = resid_ref[...] - alpha * image
        norm_next = jnp.sum(resid * resid, axis=-1, keepdims=True)
        resid_ref[...] = resid
        dir_ref[...] = resid + norm_next / (norm_now + EPSILON) * direction
        return norm_next

    lax.fori_loop(0, ITERS, step, jnp.sum(resid * resid, axis=-1, keepdims=True))


VMEM = pl.BlockSpec(memory_space=pltpu.VMEM)
SMEM = pl.BlockSpec(memory_space=pltpu.SMEM)


def grant(mib):
    return pltpu.CompilerParams(vmem_limit_bytes=mib << 20)


def chain(item_factors, tile_lists, tile_weights, user_factors):
    rank = item_factors.shape[1]
    slots = tile_lists.shape[1]
    shards = lax.axis_size("item")
    users = lax.axis_size("user")
    rows_y = shards // 2
    column = [[2 * y + c for y in range(rows_y)] for c in range(2)]
    around = [[g * NEAR + j for j in range(NEAR)] for g in range(users // NEAR)]
    swap = [(i, i ^ 1) for i in range(shards)]
    place = (lax.axis_index("user") % NEAR).astype(jnp.int32).reshape(1)
    core = (lax.axis_index("item") % 2).astype(jnp.int32).reshape(1)
    held = item_factors.shape[0] // TILE

    send_a = pl.pallas_call(
        prep_kernel,
        out_shape=jax.ShapeDtypeStruct((rows_y, (held + 1) * SLICE, rank), jnp.float32),
        in_specs=[SMEM, VMEM],
        out_specs=VMEM,
        scratch_shapes=[pltpu.VMEM((rank, rank), jnp.float32)],
        compiler_params=grant(16),
        name="prep",
    )(place, item_factors)
    mine = lax.all_to_all(send_a, "item", 0, 0, tiled=True, axis_index_groups=column)
    near_lists = tile_lists
    for bit in (1, 2, 4):
        step = [(u, u ^ bit) for u in range(users)]
        near_lists = jnp.concatenate([near_lists, lax.ppermute(near_lists, "user", step)], axis=0)
    other = lax.ppermute(mine, "item", swap)
    send_b = pl.pallas_call(
        pick_kernel,
        out_shape=jax.ShapeDtypeStruct((NEAR, (slots + 1) * SLICE, rank), jnp.float32),
        in_specs=[SMEM, SMEM, SMEM, VMEM, VMEM],
        out_specs=VMEM,
        compiler_params=grant(12),
        name="pick",
    )(core, place, near_lists, mine, other)
    tiles = lax.all_to_all(send_b, "user", 0, 0, tiled=True, axis_index_groups=around)
    return pl.pallas_call(
        solve_kernel,
        out_shape=jax.ShapeDtypeStruct((TILE, rank), jnp.float32),
        in_specs=[VMEM, VMEM, VMEM],
        out_specs=VMEM,
        scratch_shapes=[
            pltpu.VMEM(((slots + 1) * TILE, 2 * rank), jnp.bfloat16),
            pltpu.VMEM((TILE, rank), jnp.float32),
            pltpu.VMEM((TILE, rank), jnp.float32),
        ],
        compiler_params=grant(24),
        name="solve",
    )(tiles, tile_weights[0], user_factors)


def solution(mesh):
    in_specs = (
        P("item", None),
        P(("item", "user"), None),
        P(("item", "user"), None, None, None),
        P(("item", "user"), None),
    )
    out_specs = P(("item", "user"), None)
    return jax.shard_map(chain, mesh=mesh, in_specs=in_specs, out_specs=out_specs, check_vma=False)
```

```python
import jax
import jax.numpy as jnp
from jax import lax
from jax.experimental import pallas as pl
from jax.experimental.pallas import tpu as pltpu
from jax.sharding import PartitionSpec as P


ITERS = 4
RIDGE_WEIGHT = 0.1
EPSILON = 1e-06
TILE = 128
NEAR = 8
SLICE = TILE // NEAR
ROWS = 8
PIECES = 2


def halves(x):
    high = x.astype(jnp.bfloat16)
    low = (x - high.astype(jnp.float32)).astype(jnp.bfloat16)
    return high, low


def quadrants(x):
    rows, cols = x.shape[0] // 2, x.shape[1] // 2
    return (x[:rows, :cols] + x[:rows, cols:]) + (x[rows:, :cols] + x[rows:, cols:])


def prep_kernel(place_ref, shard_ref, out_ref, held_ref, stage_ref, gram_ref, load_sems, slice_sem, out_sem):
    start = pl.multiple_of(place_ref[0] * SLICE, SLICE)
    rows = shard_ref.shape[0]
    tiles = rows // TILE
    part = rows // PIECES
    body, tail = pl.ds(0, tiles * SLICE), pl.ds(tiles * SLICE, SLICE)

    def load(p):
        at = pl.ds(p * part, part)
        return pltpu.make_async_copy(shard_ref.at[at], held_ref.at[at], load_sems.at[p])

    for t in range(tiles):
        pltpu.make_async_copy(
            shard_ref.at[pl.ds(t * TILE + start, SLICE)], stage_ref.at[pl.ds(t * SLICE, SLICE)], slice_sem
        ).start()
    for p in range(PIECES):
        load(p).start()
    pltpu.make_async_copy(shard_ref.at[body], stage_ref.at[body], slice_sem).wait()
    for d in range(out_ref.shape[0]):
        pltpu.make_async_copy(stage_ref.at[body], out_ref.at[d, body], out_sem).start()
    gram = None
    for p in range(PIECES):
        load(p).wait()
        both = jnp.concatenate(halves(held_ref[p * part:(p + 1) * part, :]), axis=1)
        more = lax.dot_general(
            both, both, (((0,), (0,)), ((), ())), preferred_element_type=jnp.float32
        )
        gram = more if gram is None else gram + more
    gram_ref[...] = quadrants(gram)
    stage_ref[tail, :] = gram_ref[pl.ds(start, SLICE), :]
    for d in range(out_ref.shape[0]):
        pltpu.make_async_copy(stage_ref.at[tail], out_ref.at[d, tail], out_sem).start()
    pltpu.make_async_copy(out_ref, out_ref, out_sem).wait()


def pick_kernel(place_ref, at_ref, same_ref, mine_ref, other_ref, out_ref):
    near, slots = at_ref.shape
    place = place_ref[0]
    step = (mine_ref.shape[0] // ROWS) - SLICE
    gram = None
    for y in range(ROWS):
        at = pl.ds(y * (step + SLICE) + step, SLICE)
        more = mine_ref[at, :] + other_ref[at, :]
        gram = more if gram is None else gram + more

    def one(d, _):
        to = place ^ d
        for k in range(slots):
            at = pl.ds(pl.multiple_of(at_ref[d, k], SLICE), SLICE)
            a, b = mine_ref[at, :], other_ref[at, :]
            out_ref[to, k * SLICE:(k + 1) * SLICE, :] = jnp.where(same_ref[d, k] != 0, a, b)
        out_ref[to, slots * SLICE:, :] = gram
        return 0

    lax.fori_loop(0, near, one, 0)


def solve_kernel(tiles_ref, weights_ref, start_ref, out_ref, y_ref, resid_ref, dir_ref):
    near = tiles_ref.shape[0]
    slots = weights_ref.shape[0]
    items = slots * TILE
    chunk = 2 * TILE

    for k in range(slots + 1):
        for p in range(near):
            high, low = halves(tiles_ref[p, k * SLICE:(k + 1) * SLICE, :])
            at = k * TILE + p * SLICE
            y_ref[at:at + SLICE, :TILE] = high
            y_ref[at:at + SLICE, TILE:] = low

    def wide(n):
        pair = jnp.concatenate([weights_ref[2 * n], weights_ref[2 * n + 1]], axis=1)
        return pair.astype(jnp.float32)

    def stacked(v):
        high, low = halves(v)
        return jnp.concatenate(
            [jnp.concatenate([high, high], axis=1), jnp.concatenate([low, low], axis=1)], axis=0
        )

    def scores(left, n):
        s = lax.dot_general(
            left, y_ref[n * chunk:(n + 1) * chunk, :], (((1,), (1,)), ((), ())),
            preferred_element_type=jnp.float32,
        )
        return s[:TILE] + s[TILE:]

    def ridge(left, v):
        g = lax.dot_general(
            left, y_ref[items:, :], (((1,), (1,)), ((), ())), preferred_element_type=jnp.float32
        )
        return (g[:TILE] + g[TILE:]) + RIDGE_WEIGHT * v

    def gathered(left, of):
        total = None
        for n in range(items // chunk):
            part = jnp.dot(
                jnp.concatenate(halves(of(scores(left, n), wide(n))), axis=0),
                y_ref[n * chunk:(n + 1) * chunk, :],
                preferred_element_type=jnp.float32,
            )
            total = part if total is None else total + part
        return quadrants(total)

    start = start_ref[...]
    left = stacked(start)
    resid = gathered(left, lambda s, w: 1.0 + w * (1.0 - s)) - ridge(left, start)
    out_ref[...] = start
    resid_ref[...] = resid
    dir_ref[...] = resid

    def step(_, norm_now):
        direction = dir_ref[...]
        left = stacked(direction)
        image = gathered(left, lambda s, w: s * w) + ridge(left, direction)
        alpha = norm_now / (jnp.sum(direction * image, axis=-1, keepdims=True) + EPSILON)
        out_ref[...] = out_ref[...] + alpha * direction
        resid = resid_ref[...] - alpha * image
        norm_next = jnp.sum(resid * resid, axis=-1, keepdims=True)
        resid_ref[...] = resid
        dir_ref[...] = resid + norm_next / (norm_now + EPSILON) * direction
        return norm_next

    norm = lax.fori_loop(0, ITERS - 1, step, jnp.sum(resid * resid, axis=-1, keepdims=True))
    direction = dir_ref[...]
    left = stacked(direction)
    total = None
    for n in range(items // chunk):
        s = scores(left, n)
        part = s * s * wide(n)
        total = part if total is None else total + part
    curve = total[:, :TILE] + total[:, TILE:] + direction * ridge(left, direction)
    alpha = norm / (jnp.sum(curve, axis=-1, keepdims=True) + EPSILON)
    out_ref[...] = out_ref[...] + alpha * direction


VMEM = pl.BlockSpec(memory_space=pltpu.VMEM)
SMEM = pl.BlockSpec(memory_space=pltpu.SMEM)


def grant(mib):
    return pltpu.CompilerParams(vmem_limit_bytes=mib << 20)


def chain(item_factors, tile_lists, tile_weights, user_factors):
    rank = item_factors.shape[1]
    slots = tile_lists.shape[1]
    shards = lax.axis_size("item")
    users = lax.axis_size("user")
    rows_y = shards // 2
    assert rows_y == ROWS
    column = [[2 * y + c for y in range(rows_y)] for c in range(2)]
    around = [[g * NEAR + j for j in range(NEAR)] for g in range(users // NEAR)]
    swap = [(i, i ^ 1) for i in range(shards)]
    place = (lax.axis_index("user") % NEAR).astype(jnp.int32).reshape(1)
    core = (lax.axis_index("item") % 2).astype(jnp.int32).reshape(1)
    held = item_factors.shape[0] // TILE

    send_a = pl.pallas_call(
        prep_kernel,
        out_shape=jax.ShapeDtypeStruct((rows_y, (held + 1) * SLICE, rank), jnp.float32),
        in_specs=[SMEM, pl.BlockSpec(memory_space=pltpu.MemorySpace.HBM)],
        out_specs=pl.BlockSpec(memory_space=pltpu.MemorySpace.HBM),
        scratch_shapes=[
            pltpu.VMEM(item_factors.shape, jnp.float32),
            pltpu.VMEM(((held + 1) * SLICE, rank), jnp.float32),
            pltpu.VMEM((rank, rank), jnp.float32),
            pltpu.SemaphoreType.DMA((PIECES,)),
            pltpu.SemaphoreType.DMA,
            pltpu.SemaphoreType.DMA,
        ],
        name="prep",
    )(place, item_factors)
    mine = lax.all_to_all(send_a, "item", 0, 0, tiled=True, axis_index_groups=column)
    near_lists = tile_lists
    for bit in (1, 2, 4):
        step = [(u, u ^ bit) for u in range(users)]
        near_lists = jnp.concatenate([near_lists, lax.ppermute(near_lists, "user", step)], axis=0)
    shard = near_lists // held
    at = ((shard // 2) * (held + 1) + near_lists % held) * SLICE
    same = (shard % 2 == core).astype(jnp.int32)
    other = lax.ppermute(mine, "item", swap)
    send_b = pl.pallas_call(
        pick_kernel,
        out_shape=jax.ShapeDtypeStruct((NEAR, (slots + 1) * SLICE, rank), jnp.float32),
        in_specs=[SMEM, SMEM, SMEM, VMEM, VMEM],
        out_specs=VMEM,
        compiler_params=grant(12),
        name="pick",
    )(place, at, same, mine.reshape(-1, rank), other.reshape(-1, rank))
    tiles = lax.all_to_all(send_b, "user", 0, 0, tiled=True, axis_index_groups=around)
    return pl.pallas_call(
        solve_kernel,
        out_shape=jax.ShapeDtypeStruct((TILE, rank), jnp.float32),
        in_specs=[VMEM, VMEM, VMEM],
        out_specs=VMEM,
        scratch_shapes=[
            pltpu.VMEM(((slots + 1) * TILE, 2 * rank), jnp.bfloat16),
            pltpu.VMEM((TILE, rank), jnp.float32),
            pltpu.VMEM((TILE, rank), jnp.float32),
        ],
        compiler_params=grant(24),
        name="solve",
    )(tiles, tile_weights[0], user_factors)


def solution(mesh):
    in_specs = (
        P("item", None),
        P(("item", "user"), None),
        P(("item", "user"), None, None, None),
        P(("item", "user"), None),
    )
    out_specs = P(("item", "user"), None)
    return jax.shard_map(chain, mesh=mesh, in_specs=in_specs, out_specs=out_specs, check_vma=False)
```

```python
import jax
import jax.numpy as jnp
from jax import lax
from jax.experimental import pallas as pl
from jax.experimental.pallas import tpu as pltpu
from jax.sharding import PartitionSpec as P


ITERS = 4
RIDGE_WEIGHT = 0.1
EPSILON = 1e-06
TILE = 128
ROWS = 8
PLANE = 8
NEAR = 2 * PLANE
SLICE = TILE // NEAR
PIECES = 2


def halves(x):
    high = x.astype(jnp.bfloat16)
    low = (x - high.astype(jnp.float32)).astype(jnp.bfloat16)
    return high, low


def quadrants(x):
    rows, cols = x.shape[0] // 2, x.shape[1] // 2
    return (x[:rows, :cols] + x[:rows, cols:]) + (x[rows:, :cols] + x[rows:, cols:])


def prep_kernel(place_ref, shard_ref, out_ref, held_ref, stage_ref, gram_ref, load_sems, slice_sem, out_sem):
    rows = shard_ref.shape[0]
    tiles = rows // TILE
    part = rows // PIECES
    body, tail = pl.ds(0, tiles * SLICE), pl.ds(tiles * SLICE, SLICE)
    starts = [pl.multiple_of((b * PLANE + place_ref[0]) * SLICE, SLICE) for b in range(2)]

    def load(p):
        at = pl.ds(p * part, part)
        return pltpu.make_async_copy(shard_ref.at[at], held_ref.at[at], load_sems.at[p])

    for b in range(2):
        for t in range(tiles):
            pltpu.make_async_copy(
                shard_ref.at[pl.ds(t * TILE + starts[b], SLICE)],
                stage_ref.at[b, pl.ds(t * SLICE, SLICE)],
                slice_sem,
            ).start()
    for p in range(PIECES):
        load(p).start()
    pltpu.make_async_copy(stage_ref.at[:, body], stage_ref.at[:, body], slice_sem).wait()
    for d in range(ROWS):
        pltpu.make_async_copy(stage_ref.at[d % 2, body], out_ref.at[d, body], out_sem).start()
    gram = None
    for p in range(PIECES):
        load(p).wait()
        both = jnp.concatenate(halves(held_ref[p * part:(p + 1) * part, :]), axis=1)
        more = lax.dot_general(
            both, both, (((0,), (0,)), ((), ())), preferred_element_type=jnp.float32
        )
        gram = more if gram is None else gram + more
    gram_ref[...] = quadrants(gram)
    for b in range(2):
        stage_ref[b, tail, :] = gram_ref[pl.ds(starts[b], SLICE), :]
    for d in range(ROWS):
        pltpu.make_async_copy(stage_ref.at[d % 2, tail], out_ref.at[d, tail], out_sem).start()
    pltpu.make_async_copy(out_ref, out_ref, out_sem).wait()


def pick_kernel(place_ref, at_ref, same_ref, mine_ref, other_ref, out_ref):
    near, slots = at_ref.shape
    place = place_ref[0]
    block = mine_ref.shape[0] // ROWS
    gram = None
    for y in range(ROWS):
        at = pl.ds((y + 1) * block - SLICE, SLICE)
        more = mine_ref[at, :] + other_ref[at, :]
        gram = more if gram is None else gram + more

    def one(m, _):
        to = place ^ (((m & 1) << 3) | ((m >> 1) & 3) | ((m >> 3) << 2))
        for k in range(slots):
            at = pl.ds(pl.multiple_of(at_ref[m, k], SLICE), SLICE)
            a, b = mine_ref[at, :], other_ref[at, :]
            out_ref[to, k * SLICE:(k + 1) * SLICE, :] = jnp.where(same_ref[m, k] != 0, a, b)
        out_ref[to, slots * SLICE:, :] = gram
        return 0

    lax.fori_loop(0, near, one, 0)


def solve_kernel(tiles_ref, weights_ref, start_ref, out_ref, y_ref, resid_ref, dir_ref):
    near = tiles_ref.shape[0]
    slots = weights_ref.shape[0]
    items = slots * TILE
    chunk = 2 * TILE

    for k in range(slots + 1):
        rows = slice(k * SLICE, (k + 1) * SLICE)
        for p in range(0, near, 2):
            pair = jnp.concatenate([tiles_ref[p, rows, :], tiles_ref[p + 1, rows, :]], axis=0)
            high, low = halves(pair)
            at = k * TILE + p * SLICE
            y_ref[at:at + 2 * SLICE, :TILE] = high
            y_ref[at:at + 2 * SLICE, TILE:] = low

    def wide(n):
        pair = jnp.concatenate([weights_ref[2 * n], weights_ref[2 * n + 1]], axis=1)
        return pair.astype(jnp.float32)

    def stacked(v):
        high, low = halves(v)
        return jnp.concatenate(
            [jnp.concatenate([high, high], axis=1), jnp.concatenate([low, low], axis=1)], axis=0
        )

    def scores(left, n):
        s = lax.dot_general(
            left, y_ref[n * chunk:(n + 1) * chunk, :], (((1,), (1,)), ((), ())),
            preferred_element_type=jnp.float32,
        )
        return s[:TILE] + s[TILE:]

    def ridge(left, v):
        g = lax.dot_general(
            left, y_ref[items:, :], (((1,), (1,)), ((), ())), preferred_element_type=jnp.float32
        )
        return (g[:TILE] + g[TILE:]) + RIDGE_WEIGHT * v

    def gathered(left, of):
        total = None
        for n in range(items // chunk):
            part = jnp.dot(
                jnp.concatenate(halves(of(scores(left, n), wide(n))), axis=0),
                y_ref[n * chunk:(n + 1) * chunk, :],
                preferred_element_type=jnp.float32,
            )
            total = part if total is None else total + part
        return quadrants(total)

    start = start_ref[...]
    left = stacked(start)
    resid = gathered(left, lambda s, w: 1.0 + w * (1.0 - s)) - ridge(left, start)
    out_ref[...] = start
    resid_ref[...] = resid
    dir_ref[...] = resid

    def step(_, norm_now):
        direction = dir_ref[...]
        left = stacked(direction)
        image = gathered(left, lambda s, w: s * w) + ridge(left, direction)
        alpha = norm_now / (jnp.sum(direction * image, axis=-1, keepdims=True) + EPSILON)
        out_ref[...] = out_ref[...] + alpha * direction
        resid = resid_ref[...] - alpha * image
        norm_next = jnp.sum(resid * resid, axis=-1, keepdims=True)
        resid_ref[...] = resid
        dir_ref[...] = resid + norm_next / (norm_now + EPSILON) * direction
        return norm_next

    norm = lax.fori_loop(0, ITERS - 1, step, jnp.sum(resid * resid, axis=-1, keepdims=True))
    direction = dir_ref[...]
    left = stacked(direction)
    total = None
    for n in range(items // chunk):
        s = scores(left, n)
        part = s * s * wide(n)
        total = part if total is None else total + part
    curve = total[:, :TILE] + total[:, TILE:] + direction * ridge(left, direction)
    alpha = norm / (jnp.sum(curve, axis=-1, keepdims=True) + EPSILON)
    out_ref[...] = out_ref[...] + alpha * direction


VMEM = pl.BlockSpec(memory_space=pltpu.VMEM)
SMEM = pl.BlockSpec(memory_space=pltpu.SMEM)


def grant(mib):
    return pltpu.CompilerParams(vmem_limit_bytes=mib << 20)


def chain(item_factors, tile_lists, tile_weights, user_factors):
    rank = item_factors.shape[1]
    slots = tile_lists.shape[1]
    shards = lax.axis_size("item")
    users = lax.axis_size("user")
    assert shards == 2 * ROWS and users % PLANE == 0
    column = [[2 * y + c for y in range(ROWS)] for c in range(2)]
    around = [
        [(2 * (y + b) + c) * users + z * PLANE + r for b in range(2) for r in range(PLANE)]
        for y in range(0, ROWS, 2) for c in range(2) for z in range(users // PLANE)
    ]
    swap = [(i, i ^ 1) for i in range(shards)]
    item, user = lax.axis_index("item"), lax.axis_index("user")
    core = item & 1
    beside = (user & (PLANE - 1)).reshape(1)
    place = (((item >> 1) & 1) * PLANE + (user & (PLANE - 1))).reshape(1)
    held = item_factors.shape[0] // TILE

    pair_lists = jnp.concatenate(
        [tile_lists, lax.ppermute(tile_lists, "item", [(i, i ^ 2) for i in range(shards)])], axis=0
    )
    send_a = pl.pallas_call(
        prep_kernel,
        out_shape=jax.ShapeDtypeStruct((ROWS, (held + 1) * SLICE, rank), jnp.float32),
        in_specs=[SMEM, pl.BlockSpec(memory_space=pltpu.MemorySpace.HBM)],
        out_specs=pl.BlockSpec(memory_space=pltpu.MemorySpace.HBM),
        scratch_shapes=[
            pltpu.VMEM(item_factors.shape, jnp.float32),
            pltpu.VMEM((2, (held + 1) * SLICE, rank), jnp.float32),
            pltpu.VMEM((rank, rank), jnp.float32),
            pltpu.SemaphoreType.DMA((PIECES,)),
            pltpu.SemaphoreType.DMA,
            pltpu.SemaphoreType.DMA,
        ],
        name="prep",
    )(beside, item_factors)
    mine = lax.all_to_all(send_a, "item", 0, 0, tiled=True, axis_index_groups=column)
    quad = [pair_lists] + [
        lax.ppermute(pair_lists, "user", [(u, u ^ x) for u in range(users)]) for x in range(1, 4)
    ]
    quad = jnp.concatenate(quad, axis=0)
    near_lists = jnp.concatenate(
        [quad, lax.ppermute(quad, "user", [(u, u ^ 4) for u in range(users)])], axis=0
    )
    shard = near_lists // held
    at = ((shard // 2) * (held + 1) + near_lists % held) * SLICE
    same = (shard % 2 == core).astype(jnp.int32)
    other = lax.ppermute(mine, "item", swap)
    send_b = pl.pallas_call(
        pick_kernel,
        out_shape=jax.ShapeDtypeStruct((NEAR, (slots + 1) * SLICE, rank), jnp.float32),
        in_specs=[SMEM, SMEM, SMEM, VMEM, VMEM],
        out_specs=VMEM,
        compiler_params=grant(12),
        name="pick",
    )(place, at, same, mine.reshape(-1, rank), other.reshape(-1, rank))
    tiles = lax.all_to_all(send_b, ("item", "user"), 0, 0, tiled=True, axis_index_groups=around)
    return pl.pallas_call(
        solve_kernel,
        out_shape=jax.ShapeDtypeStruct((TILE, rank), jnp.float32),
        in_specs=[VMEM, VMEM, VMEM],
        out_specs=VMEM,
        scratch_shapes=[
            pltpu.VMEM(((slots + 1) * TILE, 2 * rank), jnp.bfloat16),
            pltpu.VMEM((TILE, rank), jnp.float32),
            pltpu.VMEM((TILE, rank), jnp.float32),
        ],
        compiler_params=grant(24),
        name="solve",
    )(tiles, tile_weights[0], user_factors)


def solution(mesh):
    in_specs = (
        P("item", None),
        P(("item", "user"), None),
        P(("item", "user"), None, None, None),
        P(("item", "user"), None),
    )
    out_specs = P(("item", "user"), None)
    return jax.shard_map(chain, mesh=mesh, in_specs=in_specs, out_specs=out_specs, check_vma=False)
```

```python
import jax
import jax.numpy as jnp
from jax import lax
from jax.experimental import pallas as pl
from jax.experimental.pallas import tpu as pltpu
from jax.sharding import PartitionSpec as P


ITERS = 4
RIDGE_WEIGHT = 0.1
EPSILON = 1e-06
TILE = 128
ROWS = 8
PLANE = 8
NEAR = 2 * PLANE
SLICE = TILE // NEAR


def halves(x):
    high = x.astype(jnp.bfloat16)
    low = (x - high.astype(jnp.float32)).astype(jnp.bfloat16)
    return high, low


def quadrants(x):
    rows, cols = x.shape[0] // 2, x.shape[1] // 2
    return (x[:rows, :cols] + x[:rows, cols:]) + (x[rows:, :cols] + x[rows:, cols:])


def prep_kernel(place_ref, shard_ref, out_ref, stage_ref, gram_ref, out_sem):
    rows = shard_ref.shape[0]
    tiles = rows // TILE
    body, tail = pl.ds(0, tiles * SLICE), pl.ds(tiles * SLICE, SLICE)
    starts = [pl.multiple_of((b * PLANE + place_ref[0]) * SLICE, SLICE) for b in range(2)]

    for b in range(2):
        for t in range(tiles):
            stage_ref[b, t * SLICE:(t + 1) * SLICE, :] = shard_ref[pl.ds(t * TILE + starts[b], SLICE), :]
    for d in range(ROWS):
        pltpu.make_async_copy(stage_ref.at[d % 2, body], out_ref.at[d, body], out_sem).start()
    both = jnp.concatenate(halves(shard_ref[...]), axis=1)
    gram = lax.dot_general(both, both, (((0,), (0,)), ((), ())), preferred_element_type=jnp.float32)
    gram_ref[...] = quadrants(gram)
    for b in range(2):
        stage_ref[b, tail, :] = gram_ref[pl.ds(starts[b], SLICE), :]
    for d in range(ROWS):
        pltpu.make_async_copy(stage_ref.at[d % 2, tail], out_ref.at[d, tail], out_sem).start()
    pltpu.make_async_copy(out_ref, out_ref, out_sem).wait()


def pick_kernel(place_ref, at_ref, mine_ref, other_ref, out_ref, both_ref):
    near, slots = at_ref.shape
    place = place_ref[0]
    rows = mine_ref.shape[0]
    block = rows // ROWS
    both_ref[:rows, :] = mine_ref[...]
    both_ref[rows:, :] = other_ref[...]
    gram = None
    for y in range(2 * ROWS):
        more = both_ref[(y + 1) * block - SLICE:(y + 1) * block, :]
        gram = more if gram is None else gram + more

    def one(m, _):
        to = place ^ (((m & 1) << 3) | ((m >> 1) & 3) | ((m >> 3) << 2))
        for k in range(slots):
            at = pl.ds(pl.multiple_of(at_ref[m, k], SLICE), SLICE)
            out_ref[to, k * SLICE:(k + 1) * SLICE, :] = both_ref[at, :]
        out_ref[to, slots * SLICE:, :] = gram
        return 0

    lax.fori_loop(0, near, one, 0)


def solve_kernel(tiles_ref, weights_ref, start_ref, out_ref, y_ref, resid_ref, dir_ref):
    near = tiles_ref.shape[0]
    slots = weights_ref.shape[0]
    items = slots * TILE
    chunk = 2 * TILE

    for k in range(slots + 1):
        rows = slice(k * SLICE, (k + 1) * SLICE)
        for p in range(0, near, 2):
            pair = jnp.concatenate([tiles_ref[p, rows, :], tiles_ref[p + 1, rows, :]], axis=0)
            high, low = halves(pair)
            at = k * TILE + p * SLICE
            y_ref[at:at + 2 * SLICE, :TILE] = high
            y_ref[at:at + 2 * SLICE, TILE:] = low

    def wide(n):
        pair = jnp.concatenate([weights_ref[2 * n], weights_ref[2 * n + 1]], axis=1)
        return pair.astype(jnp.float32)

    def stacked(v):
        high, low = halves(v)
        return jnp.concatenate(
            [jnp.concatenate([high, high], axis=1), jnp.concatenate([low, low], axis=1)], axis=0
        )

    def scores(left, n):
        s = lax.dot_general(
            left, y_ref[n * chunk:(n + 1) * chunk, :], (((1,), (1,)), ((), ())),
            preferred_element_type=jnp.float32,
        )
        return s[:TILE] + s[TILE:]

    def ridge(left, v):
        g = lax.dot_general(
            left, y_ref[items:, :], (((1,), (1,)), ((), ())), preferred_element_type=jnp.float32
        )
        return (g[:TILE] + g[TILE:]) + RIDGE_WEIGHT * v

    def gathered(left, of):
        total = None
        for n in range(items // chunk):
            part = jnp.dot(
                jnp.concatenate(halves(of(scores(left, n), wide(n))), axis=0),
                y_ref[n * chunk:(n + 1) * chunk, :],
                preferred_element_type=jnp.float32,
            )
            total = part if total is None else total + part
        return quadrants(total)

    start = start_ref[...]
    left = stacked(start)
    resid = gathered(left, lambda s, w: 1.0 + w * (1.0 - s)) - ridge(left, start)
    out_ref[...] = start
    resid_ref[...] = resid
    dir_ref[...] = resid

    def step(_, norm_now):
        direction = dir_ref[...]
        left = stacked(direction)
        image = gathered(left, lambda s, w: s * w) + ridge(left, direction)
        alpha = norm_now / (jnp.sum(direction * image, axis=-1, keepdims=True) + EPSILON)
        out_ref[...] = out_ref[...] + alpha * direction
        resid = resid_ref[...] - alpha * image
        norm_next = jnp.sum(resid * resid, axis=-1, keepdims=True)
        resid_ref[...] = resid
        dir_ref[...] = resid + norm_next / (norm_now + EPSILON) * direction
        return norm_next

    norm = lax.fori_loop(0, ITERS - 1, step, jnp.sum(resid * resid, axis=-1, keepdims=True))
    direction = dir_ref[...]
    left = stacked(direction)
    total = None
    for n in range(items // chunk):
        s = scores(left, n)
        part = s * s * wide(n)
        total = part if total is None else total + part
    curve = total[:, :TILE] + total[:, TILE:] + direction * ridge(left, direction)
    alpha = norm / (jnp.sum(curve, axis=-1, keepdims=True) + EPSILON)
    out_ref[...] = out_ref[...] + alpha * direction


VMEM = pl.BlockSpec(memory_space=pltpu.VMEM)
SMEM = pl.BlockSpec(memory_space=pltpu.SMEM)


def grant(mib):
    return pltpu.CompilerParams(vmem_limit_bytes=mib << 20)


def chain(item_factors, tile_lists, tile_weights, user_factors):
    rank = item_factors.shape[1]
    slots = tile_lists.shape[1]
    shards = lax.axis_size("item")
    users = lax.axis_size("user")
    assert shards == 2 * ROWS and users % PLANE == 0
    column = [[2 * y + c for y in range(ROWS)] for c in range(2)]
    around = [
        [(2 * (y + b) + c) * users + z * PLANE + r for b in range(2) for r in range(PLANE)]
        for y in range(0, ROWS, 2) for c in range(2) for z in range(users // PLANE)
    ]
    swap = [(i, i ^ 1) for i in range(shards)]
    item, user = lax.axis_index("item"), lax.axis_index("user")
    core = item & 1
    beside = (user & (PLANE - 1)).reshape(1)
    place = (((item >> 1) & 1) * PLANE + (user & (PLANE - 1))).reshape(1)
    held = item_factors.shape[0] // TILE

    pair_lists = jnp.concatenate(
        [tile_lists, lax.ppermute(tile_lists, "item", [(i, i ^ 2) for i in range(shards)])], axis=0
    )
    send_a = pl.pallas_call(
        prep_kernel,
        out_shape=jax.ShapeDtypeStruct((ROWS, (held + 1) * SLICE, rank), jnp.float32),
        in_specs=[SMEM, VMEM],
        out_specs=pl.BlockSpec(memory_space=pltpu.MemorySpace.HBM),
        scratch_shapes=[
            pltpu.VMEM((2, (held + 1) * SLICE, rank), jnp.float32),
            pltpu.VMEM((rank, rank), jnp.float32),
            pltpu.SemaphoreType.DMA,
        ],
        compiler_params=grant(16),
        name="prep",
    )(beside, item_factors)
    mine = lax.all_to_all(send_a, "item", 0, 0, tiled=True, axis_index_groups=column)
    quad = [pair_lists] + [
        lax.ppermute(pair_lists, "user", [(u, u ^ x) for u in range(users)]) for x in range(1, 4)
    ]
    quad = jnp.concatenate(quad, axis=0)
    near_lists = jnp.concatenate(
        [quad, lax.ppermute(quad, "user", [(u, u ^ 4) for u in range(users)])], axis=0
    )
    shard = near_lists // held
    half = jnp.where(shard % 2 == core, 0, ROWS)
    at = ((half + shard // 2) * (held + 1) + near_lists % held) * SLICE
    other = lax.ppermute(mine, "item", swap)
    send_b = pl.pallas_call(
        pick_kernel,
        out_shape=jax.ShapeDtypeStruct((NEAR, (slots + 1) * SLICE, rank), jnp.float32),
        in_specs=[SMEM, SMEM, VMEM, VMEM],
        out_specs=VMEM,
        scratch_shapes=[pltpu.VMEM((2 * ROWS * (held + 1) * SLICE, rank), jnp.float32)],
        compiler_params=grant(12),
        name="pick",
    )(place, at, mine.reshape(-1, rank), other.reshape(-1, rank))
    tiles = lax.all_to_all(send_b, ("item", "user"), 0, 0, tiled=True, axis_index_groups=around)
    return pl.pallas_call(
        solve_kernel,
        out_shape=jax.ShapeDtypeStruct((TILE, rank), jnp.float32),
        in_specs=[VMEM, VMEM, VMEM],
        out_specs=VMEM,
        scratch_shapes=[
            pltpu.VMEM(((slots + 1) * TILE, 2 * rank), jnp.bfloat16),
            pltpu.VMEM((TILE, rank), jnp.float32),
            pltpu.VMEM((TILE, rank), jnp.float32),
        ],
        compiler_params=grant(24),
        name="solve",
    )(tiles, tile_weights[0], user_factors)


def solution(mesh):
    in_specs = (
        P("item", None),
        P(("item", "user"), None),
        P(("item", "user"), None, None, None),
        P(("item", "user"), None),
    )
    out_specs = P(("item", "user"), None)
    return jax.shard_map(chain, mesh=mesh, in_specs=in_specs, out_specs=out_specs, check_vma=False)
```

```python
import jax
import jax.numpy as jnp
from jax import lax
from jax.experimental import pallas as pl
from jax.experimental.pallas import tpu as pltpu
from jax.sharding import PartitionSpec as P


ITERS = 4
RIDGE_WEIGHT = 0.1
EPSILON = 1e-06
TILE = 128
ROWS = 8
PLANE = 8
NEAR = 2 * PLANE
SLICE = TILE // NEAR


def halves(x):
    high = x.astype(jnp.bfloat16)
    low = (x - high.astype(jnp.float32)).astype(jnp.bfloat16)
    return high, low


def quadrants(x):
    rows, cols = x.shape[0] // 2, x.shape[1] // 2
    return (x[:rows, :cols] + x[:rows, cols:]) + (x[rows:, :cols] + x[rows:, cols:])


def prep_kernel(place_ref, shard_ref, out_ref, stage_ref, gram_ref, out_sem):
    rows = shard_ref.shape[0]
    tiles = rows // TILE
    body, tail = pl.ds(0, tiles * SLICE), pl.ds(tiles * SLICE, SLICE)
    starts = [pl.multiple_of((b * PLANE + place_ref[0]) * SLICE, SLICE) for b in range(2)]

    for b in range(2):
        for t in range(tiles):
            stage_ref[b, t * SLICE:(t + 1) * SLICE, :] = shard_ref[pl.ds(t * TILE + starts[b], SLICE), :]
    for d in range(ROWS):
        pltpu.make_async_copy(stage_ref.at[d % 2, body], out_ref.at[d, body], out_sem).start()
    both = jnp.concatenate(halves(shard_ref[...]), axis=1)
    gram = lax.dot_general(both, both, (((0,), (0,)), ((), ())), preferred_element_type=jnp.float32)
    gram_ref[...] = quadrants(gram)
    for b in range(2):
        stage_ref[b, tail, :] = gram_ref[pl.ds(starts[b], SLICE), :]
    for d in range(ROWS):
        pltpu.make_async_copy(stage_ref.at[d % 2, tail], out_ref.at[d, tail], out_sem).start()
    pltpu.make_async_copy(out_ref, out_ref, out_sem).wait()


def pick_kernel(place_ref, at_ref, mine_ref, other_ref, out_ref, both_ref):
    near, slots = at_ref.shape
    place = place_ref[0]
    rows = mine_ref.shape[0]
    block = rows // ROWS
    both_ref[:rows, :] = mine_ref[...]
    both_ref[rows:, :] = other_ref[...]
    gram = None
    for y in range(2 * ROWS):
        more = both_ref[(y + 1) * block - SLICE:(y + 1) * block, :]
        gram = more if gram is None else gram + more

    def one(m, _):
        to = place ^ (((m & 1) << 3) | ((m >> 1) & 3) | ((m >> 3) << 2))
        for k in range(slots):
            at = pl.ds(pl.multiple_of(at_ref[m, k], SLICE), SLICE)
            out_ref[to, k * SLICE:(k + 1) * SLICE, :] = both_ref[at, :]
        out_ref[to, slots * SLICE:, :] = gram
        return 0

    lax.fori_loop(0, near, one, 0)


def relay_kernel(lists_ref, out_ref):
    out_ref[...] = lists_ref[...]


def solve_kernel(tiles_ref, weights_ref, start_ref, out_ref, y_ref, resid_ref, dir_ref):
    near = tiles_ref.shape[0]
    slots = weights_ref.shape[0]
    items = slots * TILE
    chunk = 2 * TILE

    for k in range(slots + 1):
        rows = slice(k * SLICE, (k + 1) * SLICE)
        for p in range(0, near, 2):
            pair = jnp.concatenate([tiles_ref[p, rows, :], tiles_ref[p + 1, rows, :]], axis=0)
            high, low = halves(pair)
            at = k * TILE + p * SLICE
            y_ref[at:at + 2 * SLICE, :TILE] = high
            y_ref[at:at + 2 * SLICE, TILE:] = low

    def wide(n):
        pair = jnp.concatenate([weights_ref[2 * n], weights_ref[2 * n + 1]], axis=1)
        return pair.astype(jnp.float32)

    def stacked(v):
        high, low = halves(v)
        return jnp.concatenate(
            [jnp.concatenate([high, high], axis=1), jnp.concatenate([low, low], axis=1)], axis=0
        )

    def scores(left, n):
        s = lax.dot_general(
            left, y_ref[n * chunk:(n + 1) * chunk, :], (((1,), (1,)), ((), ())),
            preferred_element_type=jnp.float32,
        )
        return s[:TILE] + s[TILE:]

    def ridge(left, v):
        g = lax.dot_general(
            left, y_ref[items:, :], (((1,), (1,)), ((), ())), preferred_element_type=jnp.float32
        )
        return (g[:TILE] + g[TILE:]) + RIDGE_WEIGHT * v

    def gathered(left, of):
        total = None
        for n in range(items // chunk):
            part = jnp.dot(
                jnp.concatenate(halves(of(scores(left, n), wide(n))), axis=0),
                y_ref[n * chunk:(n + 1) * chunk, :],
                preferred_element_type=jnp.float32,
            )
            total = part if total is None else total + part
        return quadrants(total)

    start = start_ref[...]
    left = stacked(start)
    resid = gathered(left, lambda s, w: 1.0 + w * (1.0 - s)) - ridge(left, start)
    out_ref[...] = start
    resid_ref[...] = resid
    dir_ref[...] = resid

    def step(_, norm_now):
        direction = dir_ref[...]
        left = stacked(direction)
        image = gathered(left, lambda s, w: s * w) + ridge(left, direction)
        alpha = norm_now / (jnp.sum(direction * image, axis=-1, keepdims=True) + EPSILON)
        out_ref[...] = out_ref[...] + alpha * direction
        resid = resid_ref[...] - alpha * image
        norm_next = jnp.sum(resid * resid, axis=-1, keepdims=True)
        resid_ref[...] = resid
        dir_ref[...] = resid + norm_next / (norm_now + EPSILON) * direction
        return norm_next

    norm = lax.fori_loop(0, ITERS - 1, step, jnp.sum(resid * resid, axis=-1, keepdims=True))
    direction = dir_ref[...]
    left = stacked(direction)
    total = None
    for n in range(items // chunk):
        s = scores(left, n)
        part = s * s * wide(n)
        total = part if total is None else total + part
    curve = total[:, :TILE] + total[:, TILE:] + direction * ridge(left, direction)
    alpha = norm / (jnp.sum(curve, axis=-1, keepdims=True) + EPSILON)
    out_ref[...] = out_ref[...] + alpha * direction


VMEM = pl.BlockSpec(memory_space=pltpu.VMEM)
SMEM = pl.BlockSpec(memory_space=pltpu.SMEM)


def grant(mib):
    return pltpu.CompilerParams(vmem_limit_bytes=mib << 20)


def chain(item_factors, tile_lists, tile_weights, user_factors):
    rank = item_factors.shape[1]
    slots = tile_lists.shape[1]
    shards = lax.axis_size("item")
    users = lax.axis_size("user")
    assert shards == 2 * ROWS and users % PLANE == 0
    column = [[2 * y + c for y in range(ROWS)] for c in range(2)]
    around = [
        [(2 * (y + b) + c) * users + z * PLANE + r for b in range(2) for r in range(PLANE)]
        for y in range(0, ROWS, 2) for c in range(2) for z in range(users // PLANE)
    ]
    swap = [(i, i ^ 1) for i in range(shards)]
    item, user = lax.axis_index("item"), lax.axis_index("user")
    core = item & 1
    beside = (user & (PLANE - 1)).reshape(1)
    place = (((item >> 1) & 1) * PLANE + (user & (PLANE - 1))).reshape(1)
    held = item_factors.shape[0] // TILE

    tile_lists = pl.pallas_call(
        relay_kernel,
        out_shape=jax.ShapeDtypeStruct(tile_lists.shape, tile_lists.dtype),
        in_specs=[VMEM],
        out_specs=VMEM,
        cost_estimate=pl.CostEstimate(flops=4 << 30, bytes_accessed=8 << 20, transcendentals=0),
        compiler_params=grant(4),
        name="relay",
    )(tile_lists)
    pair_lists = jnp.concatenate(
        [tile_lists, lax.ppermute(tile_lists, "item", [(i, i ^ 2) for i in range(shards)])], axis=0
    )
    send_a = pl.pallas_call(
        prep_kernel,
        out_shape=jax.ShapeDtypeStruct((ROWS, (held + 1) * SLICE, rank), jnp.float32),
        in_specs=[SMEM, VMEM],
        out_specs=pl.BlockSpec(memory_space=pltpu.MemorySpace.HBM),
        scratch_shapes=[
            pltpu.VMEM((2, (held + 1) * SLICE, rank), jnp.float32),
            pltpu.VMEM((rank, rank), jnp.float32),
            pltpu.SemaphoreType.DMA,
        ],
        compiler_params=grant(16),
        name="prep",
    )(beside, item_factors)
    mine = lax.all_to_all(send_a, "item", 0, 0, tiled=True, axis_index_groups=column)
    quad = [pair_lists] + [
        lax.ppermute(pair_lists, "user", [(u, u ^ x) for u in range(users)]) for x in range(1, 4)
    ]
    quad = jnp.concatenate(quad, axis=0)
    near_lists = jnp.concatenate(
        [quad, lax.ppermute(quad, "user", [(u, u ^ 4) for u in range(users)])], axis=0
    )
    shard = near_lists // held
    half = jnp.where(shard % 2 == core, 0, ROWS)
    at = ((half + shard // 2) * (held + 1) + near_lists % held) * SLICE
    other = lax.ppermute(mine, "item", swap)
    send_b = pl.pallas_call(
        pick_kernel,
        out_shape=jax.ShapeDtypeStruct((NEAR, (slots + 1) * SLICE, rank), jnp.float32),
        in_specs=[SMEM, SMEM, VMEM, VMEM],
        out_specs=VMEM,
        scratch_shapes=[pltpu.VMEM((2 * ROWS * (held + 1) * SLICE, rank), jnp.float32)],
        compiler_params=grant(12),
        name="pick",
    )(place, at, mine.reshape(-1, rank), other.reshape(-1, rank))
    tiles = lax.all_to_all(send_b, ("item", "user"), 0, 0, tiled=True, axis_index_groups=around)
    return pl.pallas_call(
        solve_kernel,
        out_shape=jax.ShapeDtypeStruct((TILE, rank), jnp.float32),
        in_specs=[VMEM, VMEM, VMEM],
        out_specs=VMEM,
        scratch_shapes=[
            pltpu.VMEM(((slots + 1) * TILE, 2 * rank), jnp.bfloat16),
            pltpu.VMEM((TILE, rank), jnp.float32),
            pltpu.VMEM((TILE, rank), jnp.float32),
        ],
        compiler_params=pltpu.CompilerParams(vmem_limit_bytes=24 << 20),
        name="solve",
    )(tiles, tile_weights[0], user_factors)


def solution(mesh):
    in_specs = (
        P("item", None),
        P(("item", "user"), None),
        P(("item", "user"), None, None, None),
        P(("item", "user"), None),
    )
    out_specs = P(("item", "user"), None)
    return jax.shard_map(chain, mesh=mesh, in_specs=in_specs, out_specs=out_specs, check_vma=False)
```

```python
import jax
import jax.numpy as jnp
from jax import lax
from jax.experimental import pallas as pl
from jax.experimental.pallas import tpu as pltpu
from jax.sharding import PartitionSpec as P


ITERS = 4
RIDGE_WEIGHT = 0.1
EPSILON = 1e-06
TILE = 128
ROWS = 8
PLANE = 8
NEAR = 2 * PLANE
SLICE = TILE // NEAR


def halves(x):
    high = x.astype(jnp.bfloat16)
    low = (x - high.astype(jnp.float32)).astype(jnp.bfloat16)
    return high, low


def quadrants(x):
    rows, cols = x.shape[0] // 2, x.shape[1] // 2
    return (x[:rows, :cols] + x[:rows, cols:]) + (x[rows:, :cols] + x[rows:, cols:])


def prep_kernel(place_ref, ticket_ref, shard_ref, out_ref, stage_ref, gram_ref, out_sem):
    rows = shard_ref.shape[0]
    tiles = rows // TILE
    body, tail = pl.ds(0, tiles * SLICE), pl.ds(tiles * SLICE, SLICE)
    starts = [pl.multiple_of((b * PLANE + place_ref[0]) * SLICE, SLICE) for b in range(2)]

    for b in range(2):
        for t in range(tiles):
            stage_ref[b, t * SLICE:(t + 1) * SLICE, :] = shard_ref[pl.ds(t * TILE + starts[b], SLICE), :]
    for d in range(ROWS):
        pltpu.make_async_copy(stage_ref.at[d % 2, body], out_ref.at[d, body], out_sem).start()
    both = jnp.concatenate(halves(shard_ref[...]), axis=1)
    gram = lax.dot_general(both, both, (((0,), (0,)), ((), ())), preferred_element_type=jnp.float32)
    gram_ref[...] = quadrants(gram)
    for b in range(2):
        stage_ref[b, tail, :] = gram_ref[pl.ds(starts[b], SLICE), :]
    for d in range(ROWS):
        pltpu.make_async_copy(stage_ref.at[d % 2, tail], out_ref.at[d, tail], out_sem).start()
    pltpu.make_async_copy(out_ref, out_ref, out_sem).wait()


def pick_kernel(place_ref, at_ref, mine_ref, other_ref, out_ref, both_ref):
    near, slots = at_ref.shape
    place = place_ref[0]
    rows = mine_ref.shape[0]
    block = rows // ROWS
    both_ref[:rows, :] = mine_ref[...]
    both_ref[rows:, :] = other_ref[...]
    gram = None
    for y in range(2 * ROWS):
        more = both_ref[(y + 1) * block - SLICE:(y + 1) * block, :]
        gram = more if gram is None else gram + more

    def one(m, _):
        to = place ^ (((m & 1) << 3) | ((m >> 1) & 3) | ((m >> 3) << 2))
        for k in range(slots):
            at = pl.ds(pl.multiple_of(at_ref[m, k], SLICE), SLICE)
            out_ref[to, k * SLICE:(k + 1) * SLICE, :] = both_ref[at, :]
        out_ref[to, slots * SLICE:, :] = gram
        return 0

    lax.fori_loop(0, near, one, 0)


def ahead_kernel(out_ref):
    out_ref[...] = jnp.zeros_like(out_ref)


def solve_kernel(tiles_ref, weights_ref, start_ref, out_ref, y_ref, resid_ref, dir_ref, part_ref):
    near = tiles_ref.shape[0]
    slots = weights_ref.shape[0]
    items = slots * TILE
    chunk = 2 * TILE

    for k in range(slots + 1):
        rows = slice(k * SLICE, (k + 1) * SLICE)
        for p in range(0, near, 2):
            pair = jnp.concatenate([tiles_ref[p, rows, :], tiles_ref[p + 1, rows, :]], axis=0)
            high, low = halves(pair)
            at = k * TILE + p * SLICE
            y_ref[at:at + 2 * SLICE, :TILE] = high
            y_ref[at:at + 2 * SLICE, TILE:] = low

    def wide(n):
        pair = jnp.concatenate([weights_ref[2 * n], weights_ref[2 * n + 1]], axis=1)
        return pair.astype(jnp.float32)

    def stacked(v):
        high, low = halves(v)
        return jnp.concatenate(
            [jnp.concatenate([high, high], axis=1), jnp.concatenate([low, low], axis=1)], axis=0
        )

    def scores(left, n):
        s = lax.dot_general(
            left, y_ref[n * chunk:(n + 1) * chunk, :], (((1,), (1,)), ((), ())),
            preferred_element_type=jnp.float32,
        )
        return s[:TILE] + s[TILE:]

    def ridge(left, v):
        g = lax.dot_general(
            left, y_ref[items:, :], (((1,), (1,)), ((), ())), preferred_element_type=jnp.float32
        )
        return (g[:TILE] + g[TILE:]) + RIDGE_WEIGHT * v

    def gathered(left, of):
        for n in range(items // chunk):
            part_ref[:, n * chunk:(n + 1) * chunk] = jnp.concatenate(
                halves(of(scores(left, n), wide(n))), axis=0
            )
        total = jnp.dot(part_ref[...], y_ref[:items, :], preferred_element_type=jnp.float32)
        return quadrants(total)

    start = start_ref[...]
    left = stacked(start)
    resid = gathered(left, lambda s, w: 1.0 + w * (1.0 - s)) - ridge(left, start)
    out_ref[...] = start
    resid_ref[...] = resid
    dir_ref[...] = resid

    def step(_, norm_now):
        direction = dir_ref[...]
        left = stacked(direction)
        image = gathered(left, lambda s, w: s * w) + ridge(left, direction)
        alpha = norm_now / (jnp.sum(direction * image, axis=-1, keepdims=True) + EPSILON)
        out_ref[...] = out_ref[...] + alpha * direction
        resid = resid_ref[...] - alpha * image
        norm_next = jnp.sum(resid * resid, axis=-1, keepdims=True)
        resid_ref[...] = resid
        dir_ref[...] = resid + norm_next / (norm_now + EPSILON) * direction
        return norm_next

    norm = lax.fori_loop(0, ITERS - 1, step, jnp.sum(resid * resid, axis=-1, keepdims=True))
    direction = dir_ref[...]
    left = stacked(direction)
    total = None
    for n in range(items // chunk):
        s = scores(left, n)
        part = s * s * wide(n)
        total = part if total is None else total + part
    curve = total[:, :TILE] + total[:, TILE:] + direction * ridge(left, direction)
    alpha = norm / (jnp.sum(curve, axis=-1, keepdims=True) + EPSILON)
    out_ref[...] = out_ref[...] + alpha * direction


VMEM = pl.BlockSpec(memory_space=pltpu.VMEM)
SMEM = pl.BlockSpec(memory_space=pltpu.SMEM)


def grant(mib):
    return pltpu.CompilerParams(vmem_limit_bytes=mib << 20)


def chain(item_factors, tile_lists, tile_weights, user_factors):
    rank = item_factors.shape[1]
    slots = tile_lists.shape[1]
    shards = lax.axis_size("item")
    users = lax.axis_size("user")
    assert shards == 2 * ROWS and users % PLANE == 0
    column = [[2 * y + c for y in range(ROWS)] for c in range(2)]
    around = [
        [(2 * (y + b) + c) * users + z * PLANE + r for b in range(2) for r in range(PLANE)]
        for y in range(0, ROWS, 2) for c in range(2) for z in range(users // PLANE)
    ]
    swap = [(i, i ^ 1) for i in range(shards)]
    item, user = lax.axis_index("item"), lax.axis_index("user")
    core = item & 1
    beside = (user & (PLANE - 1)).reshape(1)
    place = (((item >> 1) & 1) * PLANE + (user & (PLANE - 1))).reshape(1)
    held = item_factors.shape[0] // TILE

    ticket = pl.pallas_call(
        ahead_kernel,
        out_shape=jax.ShapeDtypeStruct((8, rank), jnp.float32),
        out_specs=VMEM,
        cost_estimate=pl.CostEstimate(flops=4 << 30, bytes_accessed=8 << 20, transcendentals=0),
        compiler_params=grant(4),
        name="ahead",
    )()
    pair_lists = jnp.concatenate(
        [tile_lists, lax.ppermute(tile_lists, "item", [(i, i ^ 2) for i in range(shards)])], axis=0
    )
    send_a = pl.pallas_call(
        prep_kernel,
        out_shape=jax.ShapeDtypeStruct((ROWS, (held + 1) * SLICE, rank), jnp.float32),
        in_specs=[SMEM, VMEM, VMEM],
        out_specs=pl.BlockSpec(memory_space=pltpu.MemorySpace.HBM),
        scratch_shapes=[
            pltpu.VMEM((2, (held + 1) * SLICE, rank), jnp.float32),
            pltpu.VMEM((rank, rank), jnp.float32),
            pltpu.SemaphoreType.DMA,
        ],
        compiler_params=grant(16),
        name="prep",
    )(beside, ticket, item_factors)
    mine = lax.all_to_all(send_a, "item", 0, 0, tiled=True, axis_index_groups=column)
    quad = [pair_lists] + [
        lax.ppermute(pair_lists, "user", [(u, u ^ x) for u in range(users)]) for x in range(1, 4)
    ]
    quad = jnp.concatenate(quad, axis=0)
    near_lists = jnp.concatenate(
        [quad, lax.ppermute(quad, "user", [(u, u ^ 4) for u in range(users)])], axis=0
    )
    shard = near_lists // held
    half = jnp.where(shard % 2 == core, 0, ROWS)
    at = ((half + shard // 2) * (held + 1) + near_lists % held) * SLICE
    other = lax.ppermute(mine, "item", swap)
    send_b = pl.pallas_call(
        pick_kernel,
        out_shape=jax.ShapeDtypeStruct((NEAR, (slots + 1) * SLICE, rank), jnp.float32),
        in_specs=[SMEM, SMEM, VMEM, VMEM],
        out_specs=VMEM,
        scratch_shapes=[pltpu.VMEM((2 * ROWS * (held + 1) * SLICE, rank), jnp.float32)],
        compiler_params=grant(12),
        name="pick",
    )(place, at, mine.reshape(-1, rank), other.reshape(-1, rank))
    tiles = lax.all_to_all(send_b, ("item", "user"), 0, 0, tiled=True, axis_index_groups=around)
    return pl.pallas_call(
        solve_kernel,
        out_shape=jax.ShapeDtypeStruct((TILE, rank), jnp.float32),
        in_specs=[VMEM, VMEM, VMEM],
        out_specs=VMEM,
        scratch_shapes=[
            pltpu.VMEM(((slots + 1) * TILE, 2 * rank), jnp.bfloat16),
            pltpu.VMEM((TILE, rank), jnp.float32),
            pltpu.VMEM((TILE, rank), jnp.float32),
            pltpu.VMEM((2 * TILE, slots * TILE), jnp.bfloat16),
        ],
        compiler_params=pltpu.CompilerParams(vmem_limit_bytes=24 << 20),
        name="solve",
    )(tiles, tile_weights[0], user_factors)


def solution(mesh):
    in_specs = (
        P("item", None),
        P(("item", "user"), None),
        P(("item", "user"), None, None, None),
        P(("item", "user"), None),
    )
    out_specs = P(("item", "user"), None)
    return jax.shard_map(chain, mesh=mesh, in_specs=in_specs, out_specs=out_specs, check_vma=False)
```
